32 devices in a mesh: row: 4 (over y, x), col: 4 (over z), layer: 2 (over core).
Axes of the slice: x: 2, y: 2, z: 4, core: 2. Of those that a mesh axis runs over, the one named last changes fastest.
Arguments:
- a_blocks: bfloat16 [4, 4, 2, 24, 128, 128], P('row', 'col', 'layer'), may hold values from -6 to 6
- a_cells: int32 [4, 4, 2, 24], P('row', 'col', 'layer'), may hold values from 0 to 31, as said below
- a_count: int32 [4, 4, 2], P('row', 'col', 'layer'), may hold values from 12 to 24, as said below
- b_blocks: bfloat16 [4, 4, 2, 80, 128, 128], P('row', 'col', 'layer'), may hold values from -0.125 to 0.125
- b_cells: int32 [4, 4, 2, 80], P('row', 'col', 'layer'), may hold values from 0 to 127, as said below
- b_count: int32 [4, 4, 2], P('row', 'col', 'layer'), may hold values from 40 to 80, as said below
- c_cells: int32 [4, 4, 32], P('row', 'col'), may hold values from 0 to 63, as said below
Outputs:
- c_blocks: float32 [4, 4, 32, 128, 128], P('row', 'col', 'layer')
The draws below stay inside these ranges and needn't reach their ends.
Inputs may be any that keep to these rules, and one draw needn't show every extreme that they name: `a_cells`: positions are distinct within each A panel. `a_count`: some panel is full in every draw. `b_cells`: positions are distinct within each B panel. `b_count`: some panel is full in every draw. `c_cells`: positions are distinct within each tile.
All inputs are finite; a program needn't handle non-finite values.
Results may differ from the reference program's by a relative error of at most 0.0003.
Values may be sent and summed in bfloat16 or wider, within the bound.
No kernel may reach another device: no remote copies, remote signals or barrier semaphores. Data moves between devices by JAX's collectives and lax.ppermute only.
A program may use at most 128 MiB of HBM per device.

```python
import jax
import jax.numpy as jnp
from jax import lax

BS = 128
CR = 4
CC = 16
KW = 8
CAP_A = 24
CAP_B = 80
CAP_C = 32
N_ROW = 4
N_COL = 4
N_LAYER = 2


def panel_cells(key, panels, positions, capacity):
    subkeys = jax.random.split(key, panels)
    return jax.vmap(lambda subkey: jax.random.permutation(subkey, positions)[:capacity])(subkeys).astype(jnp.int32)


def live_counts(key, capacity):
    panels = N_ROW * N_COL * N_LAYER
    drawn_counts = jax.random.randint(jax.random.fold_in(key, 1), (panels,), capacity // 2, capacity + 1)
    full_panel = jax.random.randint(jax.random.fold_in(key, 2), (), 0, panels)
    counts_out = jnp.where(jnp.arange(panels) == full_panel, capacity, drawn_counts)
    return counts_out.astype(jnp.int32).reshape(N_ROW, N_COL, N_LAYER)


def draw_a_cells(key, part):
    cell_lists = panel_cells(jax.random.fold_in(key, 101), N_ROW * N_COL * N_LAYER, CR * KW, CAP_A)
    return cell_lists.reshape(N_ROW, N_COL, N_LAYER, CAP_A)


def draw_b_cells(key, part):
    cell_lists = panel_cells(jax.random.fold_in(key, 102), N_ROW * N_COL * N_LAYER, KW * CC, CAP_B)
    return cell_lists.reshape(N_ROW, N_COL, N_LAYER, CAP_B)


def draw_c_cells(key, part):
    cell_lists = panel_cells(jax.random.fold_in(key, 103), N_ROW * N_COL, CR * CC, CAP_C)
    return cell_lists.reshape(N_ROW, N_COL, CAP_C)


def draw_a_count(key, part):
    return live_counts(jax.random.fold_in(key, 201), CAP_A)


def draw_b_count(key, part):
    return live_counts(jax.random.fold_in(key, 301), CAP_B)


def block_levels(rng, dims, cuts, low, top_value):
    gain, own = 1.0, jax.random.fold_in(rng, 6)
    for position, parts in cuts:
        draws = jnp.exp(jax.random.uniform(jax.random.fold_in(own, position), (parts,), jnp.float32, low / len(cuts), top_value / len(cuts)))
        gain = gain * jnp.repeat(draws, dims[position] // parts).reshape([-1 if axis == position else 1 for axis in range(len(dims))])
    return gain


def scatter_about(stream_key, dims, deviation, most, cuts=(), kind=jnp.bfloat16):
    factor_of = block_levels(stream_key, dims, cuts, -0.22, 0.18) if cuts else 1.0
    values = jax.random.normal(stream_key, dims, jnp.float32) * deviation * factor_of
    return jnp.minimum(jnp.maximum(values, -most), most).astype(kind)


def setup_inputs(seed: int = 0) -> dict:
    key_of = jax.random.split(jax.random.key(seed), 8)
    a_blocks = scatter_about(key_of[0], (N_ROW, N_COL, N_LAYER, CAP_A, BS, BS), 1.0, 6.0, ((0, 4), (1, 4), (2, 2)))
    a_cells = draw_a_cells(jax.random.fold_in(key_of[7], 71), 0)
    a_count = draw_a_count(jax.random.fold_in(key_of[7], 71), 0)
    b_blocks = scatter_about(key_of[3], (N_ROW, N_COL, N_LAYER, CAP_B, BS, BS), (N_LAYER * KW * BS) ** -0.5, 0.125, ((0, 4), (1, 4), (2, 2)))
    b_cells = draw_b_cells(jax.random.fold_in(key_of[7], 71), 0)
    b_count = draw_b_count(jax.random.fold_in(key_of[7], 71), 0)
    c_cells = draw_c_cells(jax.random.fold_in(key_of[7], 71), 0)
    return dict(a_blocks=a_blocks, a_cells=a_cells, a_count=a_count, b_blocks=b_blocks, b_cells=b_cells, b_count=b_count, c_cells=c_cells)


def densify(blocks, cell_list, live_count, height, breadth):
    capacity = cell_list.shape[0]
    is_live = jnp.arange(capacity, dtype=jnp.int32) < live_count
    masked = jnp.where(is_live[:, None, None], blocks, jnp.zeros((), blocks.dtype))
    filled = jnp.zeros((height * breadth,) + blocks.shape[1:], blocks.dtype)
    filled = filled.at[cell_list.astype(jnp.int32)].add(masked)
    return filled.reshape(height, breadth, blocks.shape[1], blocks.shape[2])


def stop_product(left, right):
    return jnp.einsum("ikxz,kjzy->ijxy", left.astype(jnp.float32), right.astype(jnp.float32), precision=lax.Precision.HIGHEST)


def reference(a_blocks, a_cells, a_count, b_blocks, b_cells, b_count, c_cells):
    def one_tile(flat_index):
        row_index = (flat_index // N_COL).astype(jnp.int32)
        col_index = (flat_index % N_COL).astype(jnp.int32)
        row_next = ((row_index + 1) % N_ROW).astype(jnp.int32)
        col_next = ((col_index + 1) % N_COL).astype(jnp.int32)
        summed = jnp.zeros((CAP_C, BS, BS), jnp.float32)
        for layer in range(N_LAYER):
            left_here = densify(a_blocks[row_index, col_index, layer], a_cells[row_index, col_index, layer], a_count[row_index, col_index, layer], CR, KW)
            right_here = densify(b_blocks[row_index, col_index, layer], b_cells[row_index, col_index, layer], b_count[row_index, col_index, layer], KW, CC)
            left_next = densify(a_blocks[row_next, col_index, layer], a_cells[row_next, col_index, layer], a_count[row_next, col_index, layer], CR, KW)
            right_next = densify(b_blocks[row_index, col_next, layer], b_cells[row_index, col_next, layer], b_count[row_index, col_next, layer], KW, CC)
            partial_value = stop_product(left_here, right_here) + stop_product(left_next, right_next)
            kept = jnp.take(partial_value.reshape(CR * CC, BS, BS), c_cells[row_index, col_index].astype(jnp.int32), axis=0)
            summed = summed + kept
        return summed

    tiles = lax.map(one_tile, jnp.arange(N_ROW * N_COL, dtype=jnp.int32))
    return tiles.reshape(N_ROW, N_COL, CAP_C, BS, BS)
```

```python
import functools

import jax
import jax.numpy as jnp
from jax import lax
from jax.experimental import pallas as pl
from jax.experimental.pallas import tpu as pltpu
from jax.sharding import PartitionSpec as P

CR = 4
CC = 16
KW = 8
PAIR = 2
GROUPS = CC // PAIR

ANY = pl.BlockSpec(memory_space=pl.ANY)
SMEM = pl.BlockSpec(memory_space=pltpu.SMEM)


def slot_of_cell(cell_list, live_count, cells):
    slot_ids = jnp.arange(cell_list.shape[0], dtype=jnp.int32)
    positions = jnp.arange(cells, dtype=jnp.int32)
    matches = (cell_list[None, :] == positions[:, None]) & (slot_ids[None, :] < live_count)
    return jnp.sum(jnp.where(matches, slot_ids[None, :] + 1, 0), axis=1) - 1


def fill_cell(slot, blocks, target, sem):
    @pl.when(slot >= 0)
    def _():
        pltpu.make_async_copy(blocks.at[slot], target, sem).start()

    @pl.when(slot < 0)
    def _():
        target[...] = jnp.zeros(target.shape, target.dtype)


def wait_cell(slot, blocks, target, sem):
    @pl.when(slot >= 0)
    def _():
        pltpu.make_async_copy(blocks.at[slot], target, sem).wait()


def left_cell(left, cell, bs):
    return left.at[pl.ds((cell // KW) * bs, bs), pl.ds((cell % KW) * bs, bs)]


def right_cell(right, inner, col, bs):
    start = pl.multiple_of((col % PAIR) * bs, bs)
    return right.at[col // PAIR, pl.ds(inner * bs, bs), pl.ds(start, bs)]


def kept_blocks(kept, rot, acc, outs, out_sem):
    total = sum(out.shape[0] for out in outs)
    copies = []
    for place in range(total):
        cell = kept[lax.rem(place + rot[0], total)]
        out = outs[place // outs[0].shape[0]]
        copies.append(
            pltpu.make_async_copy(
                acc.at[cell % CC, cell // CC], out.at[place % out.shape[0]], out_sem.at[place]
            )
        )
    for copy in copies:
        copy.start()
    for copy in copies:
        copy.wait()


def multiply(left, right, acc, group, bs):
    product = jnp.dot(left[...], right[group], preferred_element_type=jnp.float32)
    for half in range(PAIR):
        for row in range(CR):
            acc[group * PAIR + half, row] = product[
                row * bs : (row + 1) * bs, half * bs : (half + 1) * bs
            ]


def first_kernel(bs, layers, a_slot, b_slot, kept, rot, a_blocks, b_blocks, *refs):
    outs, dense = refs[:layers], refs[layers]
    left, right, acc, a_sem, b_sem, out_sem, dense_sem = refs[layers + 1 :]

    for cell in range(CR * KW):
        fill_cell(a_slot[cell], a_blocks, left_cell(left, cell, bs), a_sem.at[cell])

    @pl.loop(0, CC)
    def _(col):
        for inner in range(KW):
            fill_cell(
                b_slot[inner * CC + col],
                b_blocks,
                right_cell(right, inner, col, bs),
                b_sem.at[inner * CC + col],
            )

    for cell in range(CR * KW):
        wait_cell(a_slot[cell], a_blocks, left_cell(left, cell, bs), a_sem.at[cell])

    @pl.loop(0, GROUPS)
    def _(group):
        for half in range(PAIR):
            col = group * PAIR + half
            for inner in range(KW):
                wait_cell(
                    b_slot[inner * CC + col],
                    b_blocks,
                    right_cell(right, inner, col, bs),
                    b_sem.at[inner * CC + col],
                )
        multiply(left, right, acc, group, bs)

    dense_copy = pltpu.make_async_copy(right, dense, dense_sem)
    dense_copy.start()
    kept_blocks(kept, rot, acc, outs, out_sem)
    dense_copy.wait()


def second_kernel(bs, layers, a_slot, kept, rot, a_blocks, dense, *refs):
    outs = refs[:layers]
    left, right, acc, a_sem, dense_sem, out_sem = refs[layers:]

    for cell in range(CR * KW):
        fill_cell(a_slot[cell], a_blocks, left_cell(left, cell, bs), a_sem.at[cell])

    for group in range(GROUPS):
        pltpu.make_async_copy(dense.at[group], right.at[group], dense_sem.at[group]).start()

    for cell in range(CR * KW):
        wait_cell(a_slot[cell], a_blocks, left_cell(left, cell, bs), a_sem.at[cell])

    @pl.loop(0, GROUPS)
    def _(group):
        pltpu.make_async_copy(dense.at[group], right.at[group], dense_sem.at[group]).wait()
        multiply(left, right, acc, group, bs)

    kept_blocks(kept, rot, acc, outs, out_sem)


def run_first(layers, a_slot, b_slot, kept, rot, a_blocks, b_blocks):
    bs, capacity = a_blocks.shape[-1], kept.shape[0]
    share = jax.ShapeDtypeStruct((capacity // layers, bs, bs), jnp.float32)
    dense = jax.ShapeDtypeStruct((GROUPS, KW * bs, PAIR * bs), b_blocks.dtype)
    return pl.pallas_call(
        functools.partial(first_kernel, bs, layers),
        name="first_product",
        out_shape=[share] * layers + [dense],
        in_specs=[SMEM] * 4 + [ANY] * 2,
        out_specs=[ANY] * (layers + 1),
        scratch_shapes=[
            pltpu.VMEM((CR * bs, KW * bs), a_blocks.dtype),
            pltpu.VMEM(dense.shape, dense.dtype),
            pltpu.VMEM((CC, CR, bs, bs), jnp.float32),
            pltpu.SemaphoreType.DMA((CR * KW,)),
            pltpu.SemaphoreType.DMA((KW * CC,)),
            pltpu.SemaphoreType.DMA((capacity,)),
            pltpu.SemaphoreType.DMA,
        ],
        compiler_params=pltpu.CompilerParams(vmem_limit_bytes=24 << 20),
        cost_estimate=pl.CostEstimate(
            flops=2 * CR * KW * CC * bs**3, bytes_accessed=12 << 20, transcendentals=0
        ),
    )(a_slot, b_slot, kept, rot, a_blocks, b_blocks)


def run_second(layers, a_slot, kept, rot, a_blocks, dense):
    bs, capacity = a_blocks.shape[-1], kept.shape[0]
    share = jax.ShapeDtypeStruct((capacity // layers, bs, bs), jnp.float32)
    return pl.pallas_call(
        functools.partial(second_kernel, bs, layers),
        name="second_product",
        out_shape=[share] * layers,
        in_specs=[SMEM] * 3 + [ANY] * 2,
        out_specs=[ANY] * layers,
        scratch_shapes=[
            pltpu.VMEM((CR * bs, KW * bs), a_blocks.dtype),
            pltpu.VMEM(dense.shape, dense.dtype),
            pltpu.VMEM((CC, CR, bs, bs), jnp.float32),
            pltpu.SemaphoreType.DMA((CR * KW,)),
            pltpu.SemaphoreType.DMA((GROUPS,)),
            pltpu.SemaphoreType.DMA((capacity,)),
        ],
        compiler_params=pltpu.CompilerParams(vmem_limit_bytes=24 << 20),
        cost_estimate=pl.CostEstimate(
            flops=2 * CR * KW * CC * bs**3, bytes_accessed=8 << 20, transcendentals=0
        ),
    )(a_slot, kept, rot, a_blocks, dense)


def layer_sum(shares, layers):
    total = shares[0]
    for step in range(1, layers):
        perm = [(i, (i + step) % layers) for i in range(layers)]
        total = total + lax.ppermute(shares[step], "layer", perm)
    return total


def on_device(rows, cols, layers, a_blocks, a_cells, a_count, b_blocks, b_cells, b_count, c_cells):
    a_blocks, a_cells, a_count = a_blocks[0, 0, 0], a_cells[0, 0, 0], a_count[0, 0, 0]
    b_blocks, b_cells, b_count = b_blocks[0, 0, 0], b_cells[0, 0, 0], b_count[0, 0, 0]
    kept = c_cells[0, 0]

    to_b = [
        (((r + 1) % rows) * cols + c, r * cols + (c + 1) % cols)
        for r in range(rows)
        for c in range(cols)
    ]
    moved_blocks = lax.ppermute(a_blocks, ("row", "col"), to_b)
    a_slot = slot_of_cell(a_cells, a_count, CR * KW)
    moved_slot = lax.ppermute(a_slot, ("row", "col"), to_b)
    moved_kept = lax.ppermute(kept, "col", [(c, (c + 1) % cols) for c in range(cols)])

    b_slot = slot_of_cell(b_cells, b_count, KW * CC)
    rot = (lax.axis_index("layer") * (kept.shape[0] // layers)).astype(jnp.int32).reshape(1)
    *first, dense = run_first(layers, a_slot, b_slot, kept, rot, a_blocks, b_blocks)
    own = layer_sum(first, layers)
    moved_blocks, own = lax.optimization_barrier((moved_blocks, own))
    second = run_second(layers, moved_slot, moved_kept, rot, moved_blocks, dense)
    other = layer_sum(second, layers)
    back = lax.ppermute(other, "col", [(c, (c - 1) % cols) for c in range(cols)])
    return (own + back)[None, None]


def solution(mesh):
    sizes = mesh.shape
    return jax.shard_map(
        functools.partial(on_device, sizes["row"], sizes["col"], sizes["layer"]),
        mesh=mesh,
        in_specs=(
            P("row", "col", "layer", None, None, None),
            P("row", "col", "layer", None),
            P("row", "col", "layer"),
            P("row", "col", "layer", None, None, None),
            P("row", "col", "layer", None),
            P("row", "col", "layer"),
            P("row", "col", None),
        ),
        out_specs=P("row", "col", "layer", None, None),
        check_vma=False,
    )
```

```python
import functools

import jax
import jax.numpy as jnp
from jax import lax
from jax.experimental import pallas as pl
from jax.experimental.pallas import tpu as pltpu
from jax.sharding import PartitionSpec as P


CR = 4
CC = 16
KW = 8
PAIR = 2
GROUPS = CC // PAIR
SCALE = 16.0

HBM = pl.BlockSpec(memory_space=pltpu.HBM)
SMEM = pl.BlockSpec(memory_space=pltpu.SMEM)
VMEM = pl.BlockSpec(memory_space=pltpu.VMEM)


def slot_of_cell(cell_list, live_count, cells):
    slot_ids = jnp.arange(cell_list.shape[0], dtype=jnp.int32)
    positions = jnp.arange(cells, dtype=jnp.int32)
    matches = (cell_list[None, :] == positions[:, None]) & (slot_ids[None, :] < live_count)
    return jnp.sum(jnp.where(matches, slot_ids[None, :] + 1, 0), axis=1) - 1


def fill_cell(slot, blocks, target, sem):
    @pl.when(slot >= 0)
    def _():
        pltpu.make_async_copy(blocks.at[slot], target, sem).start()

    @pl.when(slot < 0)
    def _():
        target[...] = jnp.zeros(target.shape, target.dtype)


def wait_cell(slot, blocks, target, sem):
    @pl.when(slot >= 0)
    def _():
        pltpu.make_async_copy(blocks.at[slot], target, sem).wait()


def left_cell(left, cell, bs):
    return left.at[pl.ds((cell // KW) * bs, bs), pl.ds((cell % KW) * bs, bs)]


def right_cell(right, inner, col, bs):
    start = pl.multiple_of((col % PAIR) * bs, bs)
    return right.at[col // PAIR, pl.ds(inner * bs, bs), pl.ds(start, bs)]


def multiply(left, right, acc, group, bs):
    product = jnp.dot(left[...], right[group], preferred_element_type=jnp.float32)
    for half in range(PAIR):
        for row in range(CR):
            acc[group * PAIR + half, row] = product[
                row * bs : (row + 1) * bs, half * bs : (half + 1) * bs
            ]


def put_kept(kept, rot, acc, outs):
    total = sum(out.shape[0] for out in outs)
    for place in range(total):
        cell = kept[lax.rem(place + rot[0], total)]
        out = outs[place // outs[0].shape[0]]
        out[place % out.shape[0]] = acc[cell % CC, cell // CC]


def first_kernel(bs, layers, a_slot, b_slot, kept, rot, a_blocks, b_blocks, *refs):
    outs, dense = refs[:layers], refs[layers]
    left, acc, a_sem, b_sem = refs[layers + 1 :]

    for cell in range(CR * KW):
        fill_cell(a_slot[cell], a_blocks, left_cell(left, cell, bs), a_sem.at[cell])

    @pl.loop(0, CC)
    def _(col):
        for inner in range(KW):
            fill_cell(
                b_slot[inner * CC + col],
                b_blocks,
                right_cell(dense, inner, col, bs),
                b_sem.at[inner * CC + col],
            )

    for cell in range(CR * KW):
        wait_cell(a_slot[cell], a_blocks, left_cell(left, cell, bs), a_sem.at[cell])

    @pl.loop(0, GROUPS)
    def _(group):
        for half in range(PAIR):
            col = group * PAIR + half
            for inner in range(KW):
                wait_cell(
                    b_slot[inner * CC + col],
                    b_blocks,
                    right_cell(dense, inner, col, bs),
                    b_sem.at[inner * CC + col],
                )
        multiply(left, dense, acc, group, bs)

    put_kept(kept, rot, acc, outs)


def second_kernel(bs, layers, a_slot, kept, rot, a_blocks, dense, *refs):
    outs = refs[:layers]
    left, acc = refs[layers:]

    for cell in range(CR * KW):
        slot = a_slot[cell]
        block = a_blocks[jnp.maximum(slot, 0)]
        left_cell(left, cell, bs)[...] = jnp.where(slot >= 0, block, jnp.zeros_like(block))

    @pl.loop(0, GROUPS)
    def _(group):
        multiply(left, dense, acc, group, bs)

    put_kept(kept, rot, acc, outs)


def run_first(layers, a_slot, b_slot, kept, rot, a_blocks, b_blocks):
    bs, capacity = a_blocks.shape[-1], kept.shape[0]
    share = jax.ShapeDtypeStruct((capacity // layers, bs, bs), jnp.float32)
    dense = jax.ShapeDtypeStruct((GROUPS, KW * bs, PAIR * bs), b_blocks.dtype)
    return pl.pallas_call(
        functools.partial(first_kernel, bs, layers),
        name="first_product",
        out_shape=[share] * layers + [dense],
        in_specs=[SMEM] * 4 + [HBM] * 2,
        out_specs=[VMEM] * (layers + 1),
        scratch_shapes=[
            pltpu.VMEM((CR * bs, KW * bs), a_blocks.dtype),
            pltpu.VMEM((CC, CR, bs, bs), jnp.float32),
            pltpu.SemaphoreType.DMA((CR * KW,)),
            pltpu.SemaphoreType.DMA((KW * CC,)),
        ],
        compiler_params=pltpu.CompilerParams(vmem_limit_bytes=24 << 20),
        cost_estimate=pl.CostEstimate(
            flops=2 * CR * KW * CC * bs**3, bytes_accessed=12 << 20, transcendentals=0
        ),
    )(a_slot, b_slot, kept, rot, a_blocks, b_blocks)


def run_second(layers, a_slot, kept, rot, a_blocks, dense):
    bs, capacity = a_blocks.shape[-1], kept.shape[0]
    share = jax.ShapeDtypeStruct((capacity // layers, bs, bs), jnp.float32)
    return pl.pallas_call(
        functools.partial(second_kernel, bs, layers),
        name="second_product",
        out_shape=[share] * layers,
        in_specs=[SMEM] * 3 + [VMEM] * 2,
        out_specs=[VMEM] * layers,
        scratch_shapes=[
            pltpu.VMEM((CR * bs, KW * bs), a_blocks.dtype),
            pltpu.VMEM((CC, CR, bs, bs), jnp.float32),
        ],
        compiler_params=pltpu.CompilerParams(vmem_limit_bytes=24 << 20),
        cost_estimate=pl.CostEstimate(
            flops=2 * CR * KW * CC * bs**3, bytes_accessed=8 << 20, transcendentals=0
        ),
    )(a_slot, kept, rot, a_blocks, dense)


def layer_sum(shares, layers):
    total = shares[0]
    for step in range(1, layers):
        perm = [(i, (i + step) % layers) for i in range(layers)]
        total = total + lax.ppermute(shares[step], "layer", perm)
    return total


def on_device(rows, cols, layers, a_blocks, a_cells, a_count, b_blocks, b_cells, b_count, c_cells):
    a_blocks, a_cells, a_count = a_blocks[0, 0, 0], a_cells[0, 0, 0], a_count[0, 0, 0]
    b_blocks, b_cells, b_count = b_blocks[0, 0, 0], b_cells[0, 0, 0], b_count[0, 0, 0]
    kept = c_cells[0, 0]

    to_b = [
        (((r + 1) % rows) * cols + c, r * cols + (c + 1) % cols)
        for r in range(rows)
        for c in range(cols)
    ]
    a_slot = slot_of_cell(a_cells, a_count, CR * KW)
    b_slot = slot_of_cell(b_cells, b_count, KW * CC)
    rot = (lax.axis_index("layer") * (kept.shape[0] // layers)).astype(jnp.int32).reshape(1)
    to_next = [(c, (c + 1) % cols) for c in range(cols)]
    to_last = [(c, (c - 1) % cols) for c in range(cols)]
    moved_blocks = lax.ppermute(a_blocks, ("row", "col"), to_b)
    moved_slot = lax.ppermute(a_slot, ("row", "col"), to_b)
    moved_kept = lax.ppermute(kept, "col", to_next)
    *first, dense = run_first(layers, a_slot, b_slot, kept, rot, a_blocks, b_blocks)
    own = layer_sum(first, layers)
    moved_blocks, own = lax.optimization_barrier((moved_blocks, own))
    second = run_second(layers, moved_slot, moved_kept, rot, moved_blocks, dense)
    other = layer_sum(second, layers)
    sent = (other * SCALE).astype(jnp.float16)
    back = lax.ppermute(sent, "col", to_last)
    total = own + back.astype(jnp.float32) * (1.0 / SCALE)
    return total[None, None]


def solution(mesh):
    sizes = mesh.shape
    return jax.shard_map(
        functools.partial(on_device, sizes["row"], sizes["col"], sizes["layer"]),
        mesh=mesh,
        in_specs=(
            P("row", "col", "layer", None, None, None),
            P("row", "col", "layer", None),
            P("row", "col", "layer"),
            P("row", "col", "layer", None, None, None),
            P("row", "col", "layer", None),
            P("row", "col", "layer"),
            P("row", "col", None),
        ),
        out_specs=P("row", "col", "layer", None, None),
        check_vma=False,
    )
```

```python
import functools

import jax
import jax.numpy as jnp
from jax import lax
from jax.experimental import pallas as pl
from jax.experimental.pallas import tpu as pltpu
from jax.sharding import PartitionSpec as P


CR = 4
CC = 16
KW = 8
PAIR = 2
GROUPS = CC // PAIR
F16_TOP = 32768.0

HBM = pl.BlockSpec(memory_space=pltpu.HBM)
SMEM = pl.BlockSpec(memory_space=pltpu.SMEM)
VMEM = pl.BlockSpec(memory_space=pltpu.VMEM)


def fill_table(table, cell_list, count):
    for cell in range(table.shape[0]):
        table[cell] = -1

    @pl.loop(0, count[0])
    def _(slot):
        table[cell_list[slot]] = slot


def fill_cell(slot, blocks, target, sem):
    @pl.when(slot >= 0)
    def _():
        pltpu.make_async_copy(blocks.at[slot], target, sem).start()

    @pl.when(slot < 0)
    def _():
        target[...] = jnp.zeros(target.shape, target.dtype)


def wait_cell(slot, blocks, target, sem):
    @pl.when(slot >= 0)
    def _():
        pltpu.make_async_copy(blocks.at[slot], target, sem).wait()


def left_cell(left, cell, bs):
    return left.at[pl.ds((cell // KW) * bs, bs), pl.ds((cell % KW) * bs, bs)]


def right_cell(right, inner, col, bs):
    start = pl.multiple_of((col % PAIR) * bs, bs)
    return right.at[col // PAIR, pl.ds(inner * bs, bs), pl.ds(start, bs)]


def multiply(left, right, acc, group, bs):
    product = jnp.dot(left[...], right[group], preferred_element_type=jnp.float32)
    for half in range(PAIR):
        for row in range(CR):
            acc[group * PAIR + half, row] = product[
                row * bs : (row + 1) * bs, half * bs : (half + 1) * bs
            ]


def put_kept(cells, rot, acc, outs, first):
    total = cells.shape[0]
    share = total // len(outs)
    for step, out in enumerate(outs):
        for place in range(out.shape[0]):
            cell = cells[lax.rem(step * share + first + place + rot[0], total)]
            out[place] = acc[cell % CC, cell // CC]


def groups_for(cells, layers, head):
    share = cells.shape[0] // layers
    last = [(cells[layer * share + head - 1] % CC) // PAIR for layer in range(layers)]
    return functools.reduce(jnp.maximum, last) + 1


def peak(value):
    return jnp.max(jnp.abs(value.astype(jnp.float32)))


def first_kernel(bs, layers, a_cells, a_count, b_cells, b_count, cells, rot, a_blocks, b_blocks, *refs):
    outs, (dense, peaks) = refs[:layers], refs[layers : layers + 2]
    left, acc, a_slot, b_slot, a_sem, b_sem = refs[layers + 2 :]

    fill_table(a_slot, a_cells, a_count)
    fill_table(b_slot, b_cells, b_count)
    for cell in range(CR * KW):
        fill_cell(a_slot[cell], a_blocks, left_cell(left, cell, bs), a_sem.at[cell])

    @pl.loop(0, CC)
    def _(col):
        for inner in range(KW):
            fill_cell(
                b_slot[inner * CC + col],
                b_blocks,
                right_cell(dense, inner, col, bs),
                b_sem.at[inner * CC + col],
            )

    for cell in range(CR * KW):
        wait_cell(a_slot[cell], a_blocks, left_cell(left, cell, bs), a_sem.at[cell])

    def group_step(group, top):
        for half in range(PAIR):
            col = group * PAIR + half
            for inner in range(KW):
                wait_cell(
                    b_slot[inner * CC + col],
                    b_blocks,
                    right_cell(dense, inner, col, bs),
                    b_sem.at[inner * CC + col],
                )
        multiply(left, dense, acc, group, bs)
        return jnp.maximum(top, peak(dense[group]))

    peaks[0] = peak(left[...])
    peaks[1] = lax.fori_loop(0, GROUPS, group_step, jnp.float32(0))
    put_kept(cells, rot, acc, outs, 0)


def head_kernel(bs, layers, a_cells, a_count, cells, rot, a_blocks, dense, *refs):
    outs, (left, acc, a_slot) = refs[:layers], refs[layers:]
    fill_table(a_slot, a_cells, a_count)
    for cell in range(CR * KW):
        slot = a_slot[cell]
        block = a_blocks[jnp.maximum(slot, 0)]
        left_cell(left, cell, bs)[...] = jnp.where(slot >= 0, block, jnp.zeros_like(block))

    @pl.loop(0, groups_for(cells, layers, outs[0].shape[0]))
    def _(group):
        multiply(left, dense, acc, group, bs)

    put_kept(cells, rot, acc, outs, 0)


def tail_kernel(bs, layers, head, cells, rot, left, dense, acc_in, *refs):
    outs, acc = refs[:layers], refs[layers]

    @pl.loop(groups_for(cells, layers, head), GROUPS)
    def _(group):
        multiply(left, dense, acc, group, bs)

    put_kept(cells, rot, acc, outs, head)


def scatter_kernel(places, blocks, *refs):
    out, sem = refs[-2:]
    copies = [
        pltpu.make_async_copy(blocks.at[i], out.at[places[i]], sem.at[i])
        for i in range(blocks.shape[0])
    ]
    for copy in copies:
        copy.start()
    for copy in copies:
        copy.wait()


def cost(share, bytes_accessed, bs):
    flops = int(share * 2 * CR * KW * CC * bs**3)
    return pl.CostEstimate(flops=flops, bytes_accessed=bytes_accessed, transcendentals=0)


def shares(count, layers, bs):
    return [jax.ShapeDtypeStruct((count, bs, bs), jnp.float32)] * layers


def run_first(layers, a_cells, a_count, b_cells, b_count, cells, rot, a_blocks, b_blocks):
    bs = a_blocks.shape[-1]
    dense = jax.ShapeDtypeStruct((GROUPS, KW * bs, PAIR * bs), b_blocks.dtype)
    *outs, dense, peaks = pl.pallas_call(
        functools.partial(first_kernel, bs, layers),
        name="first_product",
        out_shape=shares(cells.shape[0] // layers, layers, bs)
        + [dense, jax.ShapeDtypeStruct((2,), jnp.float32)],
        in_specs=[SMEM] * 6 + [HBM] * 2,
        out_specs=[VMEM] * (layers + 1) + [SMEM],
        scratch_shapes=[
            pltpu.VMEM((CR * bs, KW * bs), a_blocks.dtype),
            pltpu.VMEM((CC, CR, bs, bs), jnp.float32),
            pltpu.SMEM((CR * KW,), jnp.int32),
            pltpu.SMEM((KW * CC,), jnp.int32),
            pltpu.SemaphoreType.DMA((CR * KW,)),
            pltpu.SemaphoreType.DMA((KW * CC,)),
        ],
        compiler_params=pltpu.CompilerParams(vmem_limit_bytes=24 << 20),
        cost_estimate=cost(1, 12 << 20, bs),
    )(a_cells, a_count, b_cells, b_count, cells, rot, a_blocks, b_blocks)
    return outs, dense, peaks


def run_head(layers, head, a_cells, a_count, cells, rot, a_blocks, dense):
    bs = a_blocks.shape[-1]
    left = jax.ShapeDtypeStruct((CR * bs, KW * bs), a_blocks.dtype)
    acc = jax.ShapeDtypeStruct((CC, CR, bs, bs), jnp.float32)
    *outs, left, acc = pl.pallas_call(
        functools.partial(head_kernel, bs, layers),
        name="head_product",
        out_shape=shares(head, layers, bs) + [left, acc],
        in_specs=[SMEM] * 4 + [VMEM] * 2,
        out_specs=[VMEM] * (layers + 2),
        scratch_shapes=[pltpu.SMEM((CR * KW,), jnp.int32)],
        compiler_params=pltpu.CompilerParams(vmem_limit_bytes=24 << 20),
        cost_estimate=cost(0.5, 4 << 20, bs),
    )(a_cells, a_count, cells, rot, a_blocks, dense)
    return outs, left, acc


def run_tail(layers, head, cells, rot, left, dense, acc):
    bs = acc.shape[-1]
    tail = cells.shape[0] // layers - head
    *outs, _ = pl.pallas_call(
        functools.partial(tail_kernel, bs, layers, head),
        name="tail_product",
        out_shape=shares(tail, layers, bs) + [jax.ShapeDtypeStruct(acc.shape, acc.dtype)],
        in_specs=[SMEM] * 2 + [VMEM] * 3,
        out_specs=[VMEM] * (layers + 1),
        input_output_aliases={4: layers},
        compiler_params=pltpu.CompilerParams(vmem_limit_bytes=24 << 20),
        cost_estimate=cost(0.5, 4 << 20, bs),
    )(cells, rot, left, dense, acc)
    return outs


def scatter_blocks(places, blocks, out, capacity):
    shape = jax.ShapeDtypeStruct((capacity,) + blocks.shape[1:], blocks.dtype)
    held = [] if out is None else [out]
    return pl.pallas_call(
        scatter_kernel,
        name="scatter_blocks",
        out_shape=shape,
        in_specs=[SMEM, VMEM] + [HBM] * len(held),
        out_specs=HBM,
        scratch_shapes=[pltpu.SemaphoreType.DMA((blocks.shape[0],))],
        input_output_aliases={2: 0} if held else {},
        compiler_params=pltpu.CompilerParams(vmem_limit_bytes=4 << 20),
    )(places, blocks, *held)


def column_order(kept, layers):
    share = kept.shape[0] // layers
    lists = kept.reshape(layers, share)
    ids = jnp.arange(share, dtype=jnp.int32)
    keys = (lists % CC) * share + ids[None, :]
    rank = jnp.sum((keys[:, None, :] < keys[:, :, None]).astype(jnp.int32), axis=2)
    at_rank = rank[:, None, :] == ids[None, :, None]
    both = jnp.stack([lists, jnp.broadcast_to(ids[None, :], lists.shape)])
    return jnp.sum(jnp.where(at_rank[None], both[:, :, None, :], 0), axis=3).reshape(2, -1)


def over_layers(combine, values, layers):
    total = values[0]
    for step in range(1, layers):
        perm = [(i, (i + step) % layers) for i in range(layers)]
        total = combine(total, lax.ppermute(values[step], "layer", perm))
    return total


def narrow(value, scale):
    return lax.reduce_precision(value * scale, 8, 10).astype(jnp.float16)


def on_device(rows, cols, layers, a_blocks, a_cells, a_count, b_blocks, b_cells, b_count, c_cells):
    a_blocks, a_cells, a_count = a_blocks[0, 0, 0], a_cells[0, 0, 0], a_count[0, 0]
    b_blocks, b_cells, b_count = b_blocks[0, 0, 0], b_cells[0, 0, 0], b_count[0, 0]
    kept = c_cells[0, 0]

    to_b = [
        (((r + 1) % rows) * cols + c, r * cols + (c + 1) % cols)
        for r in range(rows)
        for c in range(cols)
    ]
    to_next = [(c, (c + 1) % cols) for c in range(cols)]
    to_last = [(c, (c - 1) % cols) for c in range(cols)]
    share = kept.shape[0] // layers
    head = (share + 1) // 2
    inner = KW * a_blocks.shape[-1]

    moved_blocks = lax.ppermute(a_blocks, ("row", "col"), to_b)
    moved_slots = lax.ppermute((a_cells, a_count), ("row", "col"), to_b)
    cells, places = column_order(kept, layers)
    layer = lax.axis_index("layer").astype(jnp.int32)
    rot = (layer * share).reshape(1)
    own_places = lax.dynamic_slice(places, (layer * share,), (share,))
    moved_cells = lax.ppermute(cells, "col", to_next)
    first, dense, peaks = run_first(
        layers,
        a_cells,
        a_count,
        b_cells,
        b_count,
        cells,
        rot,
        pltpu.with_memory_space_constraint(a_blocks, pltpu.HBM),
        pltpu.with_memory_space_constraint(b_blocks, pltpu.HBM),
    )
    own = over_layers(jnp.add, first, layers)
    peaks = over_layers(jnp.maximum, [peaks] * layers, layers)
    moved_blocks, own, peaks = lax.optimization_barrier((moved_blocks, own, peaks))
    moved_peak = lax.ppermute(peaks[:1], ("row", "col"), to_b)
    bound = jnp.maximum(layers * inner * moved_peak * peaks[1:], 1e-30)
    heads, left, acc = run_head(layers, head, *moved_slots, moved_cells, rot, moved_blocks, dense)
    other_head = over_layers(jnp.add, heads, layers)
    back_head = lax.ppermute(narrow(other_head, F16_TOP / bound), "col", to_last)
    back_bound = lax.ppermute(bound, "col", to_last)
    tails = run_tail(layers, head, moved_cells, rot, left, dense, acc)
    other_tail = over_layers(jnp.add, tails, layers)
    back_tail = lax.ppermute(narrow(other_tail, F16_TOP / bound), "col", to_last)
    unscale = back_bound * (1.0 / F16_TOP)
    total = own[:head] + back_head.astype(jnp.float32) * unscale
    out = scatter_blocks(own_places[:head], total, None, share)
    back_tail, out = lax.optimization_barrier((back_tail, out))
    total = own[head:] + back_tail.astype(jnp.float32) * unscale
    out = scatter_blocks(own_places[head:], total, out, share)
    return out[None, None]


def solution(mesh):
    sizes = mesh.shape
    return jax.shard_map(
        functools.partial(on_device, sizes["row"], sizes["col"], sizes["layer"]),
        mesh=mesh,
        in_specs=(
            P("row", "col", "layer", None, None, None),
            P("row", "col", "layer", None),
            P("row", "col", "layer"),
            P("row", "col", "layer", None, None, None),
            P("row", "col", "layer", None),
            P("row", "col", "layer"),
            P("row", "col", None),
        ),
        out_specs=P("row", "col", "layer", None, None),
        check_vma=False,
    )
```

```python
import functools

import jax
import jax.numpy as jnp
from jax import lax
from jax.experimental import pallas as pl
from jax.experimental.pallas import tpu as pltpu
from jax.sharding import PartitionSpec as P


CR = 4
CC = 16
KW = 8
PAIR = 2
GROUPS = CC // PAIR
F16_EXPONENT = 14.0
NOTE_ROWS = 16

HBM = pl.BlockSpec(memory_space=pltpu.HBM)
SMEM = pl.BlockSpec(memory_space=pltpu.SMEM)
VMEM = pl.BlockSpec(memory_space=pltpu.VMEM)


def left_cell(left, cell, bs):
    start = pl.multiple_of((cell % KW) * bs, bs)
    return left.at[pl.ds((cell // KW) * bs, bs), pl.ds(start, bs)]


def right_cell(right, cell, bs):
    panel, inner, col = cell // (KW * CC), (cell // CC) % KW, cell % CC
    start = pl.multiple_of((col % PAIR) * bs, bs)
    group = panel * GROUPS + col // PAIR
    return right.at[group, pl.ds(pl.multiple_of(inner * bs, bs), bs), pl.ds(start, bs)]


def place_slots(blocks, cell_list, count, cells, cell_ref, sem):
    @pl.loop(0, blocks.shape[0])
    def _(slot):
        cell = jnp.where(slot < count[0], cell_list[slot], cells + slot)
        pltpu.make_async_copy(blocks.at[slot], cell_ref(cell), sem).start()


def multiply(left, right, acc, group, bs):
    product = jnp.dot(left[...], right[group], preferred_element_type=jnp.float32)
    for half in range(PAIR):
        for row in range(CR):
            acc[group * PAIR + half, row] = product[
                row * bs : (row + 1) * bs, half * bs : (half + 1) * bs
            ]


def put_kept(kept, rot, acc, outs, bs):
    total = kept.shape[0]
    share = total // len(outs)
    for step, out in enumerate(outs):
        for place in range(share):
            cell = kept[lax.rem(step * share + place + rot[0], total)]
            out[place * bs : (place + 1) * bs] = acc[cell % CC, cell // CC]
        if out.shape[0] > share * bs:
            out[share * bs :] = jnp.zeros((out.shape[0] - share * bs, bs), out.dtype)


def first_kernel(bs, layers, a_cells, a_count, b_cells, b_count, kept, rot, a_blocks, b_blocks, *refs):
    outs, dense = refs[:layers], refs[layers]
    left, acc, a_sem, b_sem = refs[layers + 1 :]

    @pl.loop(0, GROUPS)
    def _(group):
        dense[group] = jnp.zeros(dense.shape[1:], dense.dtype)

    left[...] = jnp.zeros(left.shape, left.dtype)
    place_slots(
        b_blocks, b_cells, b_count, KW * CC, lambda cell: right_cell(dense, cell, bs), b_sem
    )
    place_slots(a_blocks, a_cells, a_count, CR * KW, lambda cell: left_cell(left, cell, bs), a_sem)
    pltpu.make_async_copy(b_blocks, b_blocks, b_sem).wait()
    pltpu.make_async_copy(a_blocks, a_blocks, a_sem).wait()

    @pl.loop(0, GROUPS)
    def _(group):
        multiply(left.at[pl.ds(0, CR * bs)], dense, acc, group, bs)

    put_kept(kept, rot, acc, outs, bs)


def second_kernel(bs, layers, a_cells, a_count, kept, rot, a_blocks, dense, *refs):
    outs, (left, acc, a_slot) = refs[:layers], refs[layers:]
    for cell in range(CR * KW):
        a_slot[cell] = -1

    @pl.loop(0, a_count[0])
    def _(slot):
        a_slot[a_cells[slot]] = slot

    for cell in range(CR * KW):
        slot = a_slot[cell]
        block = a_blocks[jnp.maximum(slot, 0)]
        left_cell(left, cell, bs)[...] = jnp.where(slot >= 0, block, jnp.zeros_like(block))

    @pl.loop(0, GROUPS)
    def _(group):
        multiply(left, dense, acc, group, bs)

    put_kept(kept, rot, acc, outs, bs)


def cost(bytes_accessed, bs):
    flops = 2 * CR * KW * CC * bs**3
    return pl.CostEstimate(flops=flops, bytes_accessed=bytes_accessed, transcendentals=0)


def run_first(layers, a_cells, a_count, b_cells, b_count, kept, rot, a_blocks, b_blocks):
    bs = a_blocks.shape[-1]
    spare_a, spare_b = pl.cdiv(a_blocks.shape[0], KW), pl.cdiv(b_blocks.shape[0], KW * CC)
    share = jax.ShapeDtypeStruct((kept.shape[0] // layers * bs, bs), jnp.float32)
    dense = jax.ShapeDtypeStruct(((1 + spare_b) * GROUPS, KW * bs, PAIR * bs), b_blocks.dtype)
    *outs, dense = pl.pallas_call(
        functools.partial(first_kernel, bs, layers),
        name="first_product",
        out_shape=[share] * layers + [dense],
        in_specs=[SMEM] * 6 + [HBM] * 2,
        out_specs=[VMEM] * (layers + 1),
        scratch_shapes=[
            pltpu.VMEM(((CR + spare_a) * bs, KW * bs), a_blocks.dtype),
            pltpu.VMEM((CC, CR, bs, bs), jnp.float32),
            pltpu.SemaphoreType.DMA,
            pltpu.SemaphoreType.DMA,
        ],
        compiler_params=pltpu.CompilerParams(vmem_limit_bytes=24 << 20),
        cost_estimate=cost(12 << 20, bs),
    )(a_cells, a_count, b_cells, b_count, kept, rot, a_blocks, b_blocks)
    return outs, dense


def run_second(layers, a_cells, a_count, kept, rot, a_blocks, dense):
    bs = a_blocks.shape[-1]
    share = jax.ShapeDtypeStruct((kept.shape[0] // layers * bs + NOTE_ROWS, bs), jnp.float32)
    return pl.pallas_call(
        functools.partial(second_kernel, bs, layers),
        name="second_product",
        out_shape=[share] * layers,
        in_specs=[SMEM] * 4 + [VMEM] * 2,
        out_specs=[VMEM] * layers,
        scratch_shapes=[
            pltpu.VMEM((CR * bs, KW * bs), a_blocks.dtype),
            pltpu.VMEM((CC, CR, bs, bs), jnp.float32),
            pltpu.SMEM((CR * KW,), jnp.int32),
        ],
        compiler_params=pltpu.CompilerParams(vmem_limit_bytes=24 << 20),
        cost_estimate=cost(8 << 20, bs),
    )(a_cells, a_count, kept, rot, a_blocks, dense)


def over_layers(combine, values, layers):
    total = values[0]
    for step in range(1, layers):
        perm = [(i, (i + step) % layers) for i in range(layers)]
        total = combine(total, lax.ppermute(values[step], "layer", perm))
    return total


def narrow(value):
    top = jnp.maximum(jnp.max(jnp.abs(value)), 1e-30)
    exponent = jnp.ceil(jnp.log2(top))
    rows = lax.broadcasted_iota(jnp.int32, value.shape, 0)
    scaled = value * jnp.exp2(F16_EXPONENT - exponent)
    return jnp.where(rows < value.shape[0] - NOTE_ROWS, scaled, exponent).astype(jnp.float16)


def widen(sent):
    exponent = sent[-NOTE_ROWS:][:1].astype(jnp.float32)
    return sent[:-NOTE_ROWS].astype(jnp.float32) * jnp.exp2(exponent - F16_EXPONENT)


def on_device(rows, cols, layers, a_blocks, a_cells, a_count, b_blocks, b_cells, b_count, c_cells):
    a_blocks, a_cells, a_count = a_blocks[0, 0, 0], a_cells[0, 0, 0], a_count[0, 0]
    b_blocks, b_cells, b_count = b_blocks[0, 0, 0], b_cells[0, 0, 0], b_count[0, 0]
    kept = c_cells.reshape(-1)
    to_b = [
        (((r + 1) % rows) * cols + c, r * cols + (c + 1) % cols)
        for r in range(rows)
        for c in range(cols)
    ]
    to_next = [(c, (c + 1) % cols) for c in range(cols)]
    to_last = [(c, (c - 1) % cols) for c in range(cols)]
    share, bs = kept.shape[0] // layers, a_blocks.shape[-1]
    rot = (lax.axis_index("layer").astype(jnp.int32) * share).reshape(1)

    moved_blocks = lax.ppermute(a_blocks, ("row", "col"), to_b)
    moved_cells, moved_count = lax.ppermute((a_cells, a_count), ("row", "col"), to_b)
    moved_kept = lax.ppermute(kept, "col", to_next)
    first, dense = run_first(
        layers,
        a_cells,
        a_count,
        b_cells,
        b_count,
        kept,
        rot,
        pltpu.with_memory_space_constraint(a_blocks, pltpu.HBM),
        pltpu.with_memory_space_constraint(b_blocks, pltpu.HBM),
    )
    second = run_second(layers, moved_cells, moved_count, moved_kept, rot, moved_blocks, dense)
    other = over_layers(jnp.add, second, layers)
    back = lax.ppermute(narrow(other), "col", to_last)
    own = over_layers(jnp.add, first, layers)
    total = own + widen(back)
    return total.reshape(1, 1, share, bs, bs)


def solution(mesh):
    sizes = mesh.shape
    return jax.shard_map(
        functools.partial(on_device, sizes["row"], sizes["col"], sizes["layer"]),
        mesh=mesh,
        in_specs=(
            P("row", "col", "layer", None, None, None),
            P("row", "col", "layer", None),
            P("row", "col", "layer"),
            P("row", "col", "layer", None, None, None),
            P("row", "col", "layer", None),
            P("row", "col", "layer"),
            P("row", "col", None),
        ),
        out_specs=P("row", "col", "layer", None, None),
        check_vma=False,
    )
```

```python
import functools

import jax
import jax.numpy as jnp
from jax import lax
from jax.experimental import pallas as pl
from jax.experimental.pallas import tpu as pltpu
from jax.sharding import PartitionSpec as P


CR = 4
CC = 16
KW = 8
F16_EXPONENT = 14.0
NOTE_ROWS = 16

HBM = pl.BlockSpec(memory_space=pltpu.HBM)
SMEM = pl.BlockSpec(memory_space=pltpu.SMEM)
VMEM = pl.BlockSpec(memory_space=pltpu.VMEM)


def left_cell(left, cell, bs):
    start = pl.multiple_of((cell % KW) * bs, bs)
    return left.at[pl.ds((cell // KW) * bs, bs), pl.ds(start, bs)]


def right_cell(right, cell, bs):
    panel, inner, col = cell // (KW * CC), (cell // CC) % KW, cell % CC
    return right.at[panel * CC + col, pl.ds(pl.multiple_of(inner * bs, bs), bs)]


def place_slots(blocks, cell_list, count, cells, cell_ref, sem):
    @pl.loop(0, blocks.shape[0])
    def _(slot):
        cell = jnp.where(slot < count[0], cell_list[slot], cells + slot)
        pltpu.make_async_copy(blocks.at[slot], cell_ref(cell), sem).start()


def pair_up(kept, first, second, pending):
    for row in range(CR):
        pending[row] = -1
    count = 0
    for place in range(kept.shape[0]):
        row = kept[place] // CC
        waiting = pending[row]
        first[count], second[count] = waiting, place
        count = count + (waiting >= 0).astype(jnp.int32)
        pending[row] = jnp.where(waiting >= 0, -1, place)
    for row in range(CR):
        waiting = pending[row]
        first[count], second[count] = waiting, waiting
        count = count + (waiting >= 0).astype(jnp.int32)
    for spare in range(CR // 2):
        first[count + spare], second[count + spare] = first[0], second[0]


def pairs_of(capacity):
    return (capacity + CR) // 2


def multiply_kept(kept, rot, first, second, left, right, out, bs):
    total, layers = kept.shape[0], out.shape[0]
    share = total // layers
    top = jnp.zeros((8, bs), jnp.float32)
    for pair in range(pairs_of(total)):
        places = first[pair], second[pair]
        cells = [kept[place] for place in places]
        rows = left[pl.ds(pl.multiple_of((cells[0] // CC) * bs, bs), bs)]
        cols = jnp.concatenate([right[cell % CC] for cell in cells], axis=1)
        product = jnp.dot(rows, cols, preferred_element_type=jnp.float32)
        for half, place in enumerate(places):
            block = product[:, half * bs : (half + 1) * bs]
            to = lax.rem(place - rot[0] + total, total)
            start = pl.multiple_of((to % share) * bs, bs)
            out[to // share, pl.ds(start, bs)] = block
            top = jnp.maximum(top, jnp.max(jnp.abs(block).reshape(-1, 8, bs), axis=0))
    return top


def first_kernel(bs, a_cells, a_count, b_cells, b_count, kept, rot, a_blocks, b_blocks, *refs):
    out, dense, left, first, second, pending, a_sem, b_sem = refs

    @pl.loop(0, CC)
    def _(col):
        dense[col] = jnp.zeros(dense.shape[1:], dense.dtype)

    left[...] = jnp.zeros(left.shape, left.dtype)
    place_slots(
        b_blocks, b_cells, b_count, KW * CC, lambda cell: right_cell(dense, cell, bs), b_sem
    )
    place_slots(a_blocks, a_cells, a_count, CR * KW, lambda cell: left_cell(left, cell, bs), a_sem)
    pair_up(kept, first, second, pending)
    pltpu.make_async_copy(b_blocks, b_blocks, b_sem).wait()
    pltpu.make_async_copy(a_blocks, a_blocks, a_sem).wait()
    multiply_kept(kept, rot, first, second, left, dense, out, bs)


def second_kernel(bs, a_cells, a_count, kept, rot, a_blocks, dense, *refs):
    out, left, a_slot, first, second, pending = refs
    for cell in range(CR * KW):
        a_slot[cell] = -1

    @pl.loop(0, a_count[0])
    def _(slot):
        a_slot[a_cells[slot]] = slot

    pair_up(kept, first, second, pending)
    for cell in range(CR * KW):
        slot = a_slot[cell]
        block = a_blocks[jnp.maximum(slot, 0)]
        left_cell(left, cell, bs)[...] = jnp.where(slot >= 0, block, jnp.zeros_like(block))

    top = multiply_kept(kept, rot, first, second, left, dense, out, bs)
    for layer in range(out.shape[0]):
        for start in range(out.shape[1] - NOTE_ROWS, out.shape[1], 8):
            out[layer, start : start + 8] = top


def cost(bytes_accessed, bs):
    flops = CR * KW * CC * bs**3
    return pl.CostEstimate(flops=flops, bytes_accessed=bytes_accessed, transcendentals=0)


def pair_scratch(capacity):
    lists = pltpu.SMEM((pairs_of(capacity) + CR // 2,), jnp.int32)
    return [lists, lists, pltpu.SMEM((CR,), jnp.int32)]


def run_first(layers, a_cells, a_count, b_cells, b_count, kept, rot, a_blocks, b_blocks):
    bs = a_blocks.shape[-1]
    spare_a, spare_b = pl.cdiv(a_blocks.shape[0], KW), pl.cdiv(b_blocks.shape[0], KW * CC)
    return pl.pallas_call(
        functools.partial(first_kernel, bs),
        name="first_product",
        out_shape=[
            jax.ShapeDtypeStruct((layers, kept.shape[0] // layers * bs, bs), jnp.float32),
            jax.ShapeDtypeStruct(((1 + spare_b) * CC, KW * bs, bs), b_blocks.dtype),
        ],
        in_specs=[SMEM] * 6 + [HBM] * 2,
        out_specs=[VMEM] * 2,
        scratch_shapes=[pltpu.VMEM(((CR + spare_a) * bs, KW * bs), a_blocks.dtype)]
        + pair_scratch(kept.shape[0])
        + [pltpu.SemaphoreType.DMA] * 2,
        compiler_params=pltpu.CompilerParams(vmem_limit_bytes=20 << 20),
        cost_estimate=cost(12 << 20, bs),
    )(a_cells, a_count, b_cells, b_count, kept, rot, a_blocks, b_blocks)


def run_second(layers, a_cells, a_count, kept, rot, a_blocks, dense):
    bs = a_blocks.shape[-1]
    rows = kept.shape[0] // layers * bs + NOTE_ROWS
    return pl.pallas_call(
        functools.partial(second_kernel, bs),
        name="second_product",
        out_shape=jax.ShapeDtypeStruct((layers, rows, bs), jnp.float32),
        in_specs=[SMEM] * 4 + [VMEM] * 2,
        out_specs=VMEM,
        scratch_shapes=[
            pltpu.VMEM((CR * bs, KW * bs), a_blocks.dtype),
            pltpu.SMEM((CR * KW,), jnp.int32),
        ]
        + pair_scratch(kept.shape[0]),
        compiler_params=pltpu.CompilerParams(vmem_limit_bytes=20 << 20),
        cost_estimate=cost(8 << 20, bs),
    )(a_cells, a_count, kept, rot, a_blocks, dense)


def over_layers(combine, values, layers):
    total = values[0]
    for step in range(1, layers):
        perm = [(i, (i + step) % layers) for i in range(layers)]
        total = combine(total, lax.ppermute(values[step], "layer", perm))
    return total


def narrow(value):
    tiles = value.reshape(-1, 8, value.shape[-1])
    notes = NOTE_ROWS // 8
    exponent = jnp.ceil(jnp.log2(jnp.maximum(tiles[-1], 1e-30)))
    scaled = tiles[:-notes] * jnp.exp2(F16_EXPONENT - exponent)[None]
    noted = jnp.broadcast_to(exponent[None], (notes,) + exponent.shape)
    return jnp.concatenate([scaled, noted]).astype(jnp.float16).reshape(value.shape)


def widen(sent):
    tiles = sent.astype(jnp.float32).reshape(-1, 8, sent.shape[-1])
    scaled = tiles[: -(NOTE_ROWS // 8)] * jnp.exp2(tiles[-1] - F16_EXPONENT)[None]
    return scaled.reshape(-1, sent.shape[-1])


def on_device(rows, cols, layers, a_blocks, a_cells, a_count, b_blocks, b_cells, b_count, c_cells):
    a_blocks, a_cells, a_count = a_blocks[0, 0, 0], a_cells[0, 0, 0], a_count[0, 0]
    b_blocks, b_cells, b_count = b_blocks[0, 0, 0], b_cells[0, 0, 0], b_count[0, 0]
    kept = c_cells.reshape(-1)
    to_b = [
        (((r + 1) % rows) * cols + c, r * cols + (c + 1) % cols)
        for r in range(rows)
        for c in range(cols)
    ]
    to_next = [(c, (c + 1) % cols) for c in range(cols)]
    to_last = [(c, (c - 1) % cols) for c in range(cols)]
    share, bs = kept.shape[0] // layers, a_blocks.shape[-1]
    rot = (lax.axis_index("layer").astype(jnp.int32) * share).reshape(1)

    moved_blocks = lax.ppermute(a_blocks, ("row", "col"), to_b)
    moved_cells, moved_count = lax.ppermute((a_cells, a_count), ("row", "col"), to_b)
    moved_kept = lax.ppermute(kept, "col", to_next)
    first, dense = run_first(
        layers,
        a_cells,
        a_count,
        b_cells,
        b_count,
        kept,
        rot,
        pltpu.with_memory_space_constraint(a_blocks, pltpu.HBM),
        pltpu.with_memory_space_constraint(b_blocks, pltpu.HBM),
    )
    second = run_second(layers, moved_cells, moved_count, moved_kept, rot, moved_blocks, dense)
    other = over_layers(jnp.add, second, layers)
    back = lax.ppermute(narrow(other), "col", to_last)
    own = over_layers(jnp.add, first, layers)
    total = own + widen(back)
    return total.reshape(1, 1, share, bs, bs)


def solution(mesh):
    sizes = mesh.shape
    return jax.shard_map(
        functools.partial(on_device, sizes["row"], sizes["col"], sizes["layer"]),
        mesh=mesh,
        in_specs=(
            P("row", "col", "layer", None, None, None),
            P("row", "col", "layer", None),
            P("row", "col", "layer"),
            P("row", "col", "layer", None, None, None),
            P("row", "col", "layer", None),
            P("row", "col", "layer"),
            P("row", "col", None),
        ),
        out_specs=P("row", "col", "layer", None, None),
        check_vma=False,
    )
```

```python
import functools

import jax
import jax.numpy as jnp
from jax import lax
from jax.experimental import pallas as pl
from jax.experimental.pallas import tpu as pltpu
from jax.sharding import PartitionSpec as P


CR = 4
CC = 16
KW = 8
F16_EXPONENT = 14.0
NOTE_ROWS = 16

HBM = pl.BlockSpec(memory_space=pltpu.HBM)
SMEM = pl.BlockSpec(memory_space=pltpu.SMEM)
VMEM = pl.BlockSpec(memory_space=pltpu.VMEM)


def left_cell(left, cell, bs):
    start = pl.multiple_of((cell % KW) * bs, bs)
    return left.at[pl.ds((cell // KW) * bs, bs), pl.ds(start, bs)]


def right_cell(right, cell, bs):
    panel, inner, col = cell // (KW * CC), (cell // CC) % KW, cell % CC
    return right.at[panel * CC + col, pl.ds(pl.multiple_of(inner * bs, bs), bs)]


def place_slots(blocks, cell_list, count, cells, cell_ref, sem):
    @pl.loop(0, blocks.shape[0])
    def _(slot):
        cell = jnp.where(slot < count[0], cell_list[slot], cells + slot)
        pltpu.make_async_copy(blocks.at[slot], cell_ref(cell), sem).start()


def pair_up(kept, rot, places, first, second, pending):
    for row in range(CR):
        pending[row] = -1
    count = 0
    for place in places:
        row = kept_cell(kept, rot, place) // CC
        waiting = pending[row]
        first[count], second[count] = waiting, place
        count = count + (waiting >= 0).astype(jnp.int32)
        pending[row] = jnp.where(waiting >= 0, -1, place)
    for row in range(CR):
        waiting = pending[row]
        first[count], second[count] = waiting, waiting
        count = count + (waiting >= 0).astype(jnp.int32)
    for spare in range(most_pairs(len(places)) - pl.cdiv(len(places), 2)):
        first[count + spare], second[count + spare] = first[0], second[0]


def most_pairs(places):
    return (places + CR) // 2


def kept_cell(kept, rot, place):
    return kept[lax.rem(place + rot[0], kept.shape[0])]


def multiply_kept(kept, rot, places, lists, left, right, out, bs):
    first, second, pending = lists
    share = len(places) // out.shape[0]
    pair_up(kept, rot, places, first, second, pending)
    top = jnp.zeros((8, bs), jnp.float32)
    for pair in range(most_pairs(len(places))):
        chosen = first[pair], second[pair]
        cells = [kept_cell(kept, rot, place) for place in chosen]
        rows = left[pl.ds(pl.multiple_of((cells[0] // CC) * bs, bs), bs)]
        cols = jnp.concatenate([right[cell % CC] for cell in cells], axis=1)
        product = jnp.dot(rows, cols, preferred_element_type=jnp.float32)
        for half, place in enumerate(chosen):
            block = product[:, half * bs : (half + 1) * bs]
            to = place - places[0]
            out[to // share, pl.ds(pl.multiple_of((to % share) * bs, bs), bs)] = block
            top = jnp.maximum(top, jnp.max(jnp.abs(block).reshape(-1, 8, bs), axis=0))
    return top


def put_notes(out, top):
    for part in range(out.shape[0]):
        for start in range(out.shape[1] - NOTE_ROWS, out.shape[1], 8):
            out[part, start : start + 8] = top


def first_kernel(bs, a_cells, a_count, b_cells, b_count, kept, rot, a_blocks, b_blocks, *refs):
    out, dense, left, *lists, a_sem, b_sem = refs

    @pl.loop(0, CC)
    def _(col):
        dense[col] = jnp.zeros(dense.shape[1:], dense.dtype)

    left[...] = jnp.zeros(left.shape, left.dtype)
    place_slots(
        b_blocks, b_cells, b_count, KW * CC, lambda cell: right_cell(dense, cell, bs), b_sem
    )
    place_slots(a_blocks, a_cells, a_count, CR * KW, lambda cell: left_cell(left, cell, bs), a_sem)
    pltpu.make_async_copy(b_blocks, b_blocks, b_sem).wait()
    pltpu.make_async_copy(a_blocks, a_blocks, a_sem).wait()
    multiply_kept(kept, rot, range(kept.shape[0]), lists, left, dense, out, bs)


def others_kernel(bs, a_cells, a_count, kept, rot, a_blocks, dense, *refs):
    out, left, a_slot, *lists = refs
    for cell in range(CR * KW):
        a_slot[cell] = -1

    @pl.loop(0, a_count[0])
    def _(slot):
        a_slot[a_cells[slot]] = slot

    for cell in range(CR * KW):
        slot = a_slot[cell]
        block = a_blocks[jnp.maximum(slot, 0)]
        left_cell(left, cell, bs)[...] = jnp.where(slot >= 0, block, jnp.zeros_like(block))

    places = range(kept.shape[0] // (out.shape[0] + 1), kept.shape[0])
    put_notes(out, multiply_kept(kept, rot, places, lists, left, dense, out, bs))


def own_kernel(bs, kept, rot, left, dense, *refs):
    out, *lists = refs
    places = range((out.shape[1] - NOTE_ROWS) // bs)
    put_notes(out, multiply_kept(kept, rot, places, lists, left, dense, out, bs))


def cost(bytes_accessed, bs):
    flops = CR * KW * CC * bs**3 // 2
    return pl.CostEstimate(flops=flops, bytes_accessed=bytes_accessed, transcendentals=0)


def pair_lists(places):
    lists = pltpu.SMEM((most_pairs(places) + CR // 2,), jnp.int32)
    return [lists, lists, pltpu.SMEM((CR,), jnp.int32)]


def run_first(layers, a_cells, a_count, b_cells, b_count, kept, rot, a_blocks, b_blocks):
    bs = a_blocks.shape[-1]
    spare_a, spare_b = pl.cdiv(a_blocks.shape[0], KW), pl.cdiv(b_blocks.shape[0], KW * CC)
    return pl.pallas_call(
        functools.partial(first_kernel, bs),
        name="first_product",
        out_shape=[
            jax.ShapeDtypeStruct((layers, kept.shape[0] // layers * bs, bs), jnp.float32),
            jax.ShapeDtypeStruct(((1 + spare_b) * CC, KW * bs, bs), b_blocks.dtype),
        ],
        in_specs=[SMEM] * 6 + [HBM] * 2,
        out_specs=[VMEM] * 2,
        scratch_shapes=[pltpu.VMEM(((CR + spare_a) * bs, KW * bs), a_blocks.dtype)]
        + pair_lists(kept.shape[0])
        + [pltpu.SemaphoreType.DMA] * 2,
        compiler_params=pltpu.CompilerParams(vmem_limit_bytes=20 << 20),
        cost_estimate=cost(12 << 20, bs),
    )(a_cells, a_count, b_cells, b_count, kept, rot, a_blocks, b_blocks)


def run_others(layers, a_cells, a_count, kept, rot, a_blocks, dense):
    bs, share = a_blocks.shape[-1], kept.shape[0] // layers
    return pl.pallas_call(
        functools.partial(others_kernel, bs),
        name="others_product",
        out_shape=[
            jax.ShapeDtypeStruct((layers - 1, share * bs + NOTE_ROWS, bs), jnp.float32),
            jax.ShapeDtypeStruct((CR * bs, KW * bs), a_blocks.dtype),
        ],
        in_specs=[SMEM] * 4 + [VMEM] * 2,
        out_specs=[VMEM] * 2,
        scratch_shapes=[pltpu.SMEM((CR * KW,), jnp.int32)] + pair_lists(kept.shape[0] - share),
        compiler_params=pltpu.CompilerParams(vmem_limit_bytes=20 << 20),
        cost_estimate=cost(8 << 20, bs),
    )(a_cells, a_count, kept, rot, a_blocks, dense)


def run_own(layers, kept, rot, left, dense):
    bs, share = dense.shape[-1], kept.shape[0] // layers
    return pl.pallas_call(
        functools.partial(own_kernel, bs),
        name="own_product",
        out_shape=jax.ShapeDtypeStruct((1, share * bs + NOTE_ROWS, bs), jnp.float32),
        in_specs=[SMEM] * 2 + [VMEM] * 2,
        out_specs=VMEM,
        scratch_shapes=pair_lists(share),
        compiler_params=pltpu.CompilerParams(vmem_limit_bytes=20 << 20),
        cost_estimate=cost(8 << 20, bs),
    )(kept, rot, left, dense)


def from_layers(parts, layers):
    gained = []
    for step in range(1, layers):
        perm = [(i, (i + step) % layers) for i in range(layers)]
        gained.append(lax.ppermute(parts[step - 1], "layer", perm))
    return gained


def narrow(value):
    tiles = value.reshape(-1, 8, value.shape[-1])
    notes = NOTE_ROWS // 8
    exponent = jnp.ceil(jnp.log2(jnp.maximum(tiles[-1], 1e-30)))
    scaled = tiles[:-notes] * jnp.exp2(F16_EXPONENT - exponent)[None]
    noted = jnp.broadcast_to(exponent[None], (notes,) + exponent.shape)
    return jnp.concatenate([scaled, noted]).astype(jnp.float16).reshape(value.shape)


def widen(sent):
    tiles = sent.astype(jnp.float32).reshape(-1, 8, sent.shape[-1])
    scaled = tiles[: -(NOTE_ROWS // 8)] * jnp.exp2(tiles[-1] - F16_EXPONENT)[None]
    return scaled.reshape(-1, sent.shape[-1])


def on_device(rows, cols, layers, a_blocks, a_cells, a_count, b_blocks, b_cells, b_count, c_cells):
    a_blocks, a_cells, a_count = a_blocks[0, 0, 0], a_cells[0, 0, 0], a_count[0, 0]
    b_blocks, b_cells, b_count = b_blocks[0, 0, 0], b_cells[0, 0, 0], b_count[0, 0]
    kept = c_cells.reshape(-1)
    to_b = [
        (((r + 1) % rows) * cols + c, r * cols + (c + 1) % cols)
        for r in range(rows)
        for c in range(cols)
    ]
    to_next = [(c, (c + 1) % cols) for c in range(cols)]
    to_last = [(c, (c - 1) % cols) for c in range(cols)]
    share, bs = kept.shape[0] // layers, a_blocks.shape[-1]
    rot = (lax.axis_index("layer").astype(jnp.int32) * share).reshape(1)

    moved_blocks = lax.ppermute(a_blocks, ("row", "col"), to_b)
    moved_cells, moved_count = lax.ppermute((a_cells, a_count), ("row", "col"), to_b)
    moved_kept = lax.ppermute(kept, "col", to_next)
    first, dense = run_first(
        layers,
        a_cells,
        a_count,
        b_cells,
        b_count,
        kept,
        rot,
        pltpu.with_memory_space_constraint(a_blocks, pltpu.HBM),
        pltpu.with_memory_space_constraint(b_blocks, pltpu.HBM),
    )
    others, left = run_others(
        layers, moved_cells, moved_count, moved_kept, rot, moved_blocks, dense
    )
    gained = from_layers(others, layers)
    own = run_own(layers, moved_kept, rot, left, dense)[0]
    back = lax.ppermute(narrow(sum(gained, own)), "col", to_last)
    own = sum(from_layers(first[1:], layers), first[0])
    total = own + widen(back)
    return total.reshape(1, 1, share, bs, bs)


def solution(mesh):
    sizes = mesh.shape
    return jax.shard_map(
        functools.partial(on_device, sizes["row"], sizes["col"], sizes["layer"]),
        mesh=mesh,
        in_specs=(
            P("row", "col", "layer", None, None, None),
            P("row", "col", "layer", None),
            P("row", "col", "layer"),
            P("row", "col", "layer", None, None, None),
            P("row", "col", "layer", None),
            P("row", "col", "layer"),
            P("row", "col", None),
        ),
        out_specs=P("row", "col", "layer", None, None),
        check_vma=False,
    )
```
